32 devices in a mesh: row: 4 (over z), col: 8 (over y, x, core).
Axes of the slice: x: 2, y: 2, z: 4, core: 2. Of those that a mesh axis runs over, the one named last changes fastest.
Arguments:
- slip_load: bfloat16 [4, 8, 1024, 128], P('row', 'col'), may hold values from -6 to 6
- flexibility: bfloat16 [4, 8, 1024, 1024], P('row', 'col'), as said below
- schur: bfloat16 [4, 8, 1024, 1024], P('row', 'col'), as said below
- corner_coupling: float32 [4, 8, 12, 1024], P('row', 'col'), may hold values from -0.1875 to 0.1875
- coarse_inverse: float32 [384, 384], P('row', 'col'), as said below
- bounds_table: float32 [16], replicated, may hold values from 0.3 to 3
- bound_index: int32 [4, 8, 1024], P('row', 'col'), may hold values from 0 to 15
- face_rows: int32 [4, 8, 4], P('row', 'col'), may hold values from 0 to 256, as said below
Outputs:
- multipliers: bfloat16 [4, 8, 1024, 128], P('row', 'col')
The draws below stay inside these ranges and needn't reach their ends.
Inputs may be any that keep to these rules, and one draw needn't show every extreme that they name: `face_rows`: face counts agree between the two subdomains of a shared face, are 0 on faces at the edge of the grid, and some face has exactly 256 live slots. `coarse_inverse`: symmetric. `flexibility`: symmetric and positive definite. `schur`: symmetric and positive definite.
All inputs are finite; a program needn't handle non-finite values.
Results may differ from the reference program's by a relative error of at most 0.0038.
Values sent between devices are 32-bit elements; how exact they have to be, the bound alone decides.
No kernel may reach another device: no remote copies, remote signals or barrier semaphores. Data moves between devices by JAX's collectives and lax.ppermute only.
A program may use at most 64 MiB of HBM per device.

```python
import math
import jax
import jax.numpy as jnp
from jax import lax

M = 1024
NC = 12
R = 128
LEVELS = 16
ITERS = 2
FACE = 256
NCO = 384
N_ROW = 4
N_COL = 8


def dominant_blocks(key, spread_low, spread_high):

    def one_block(index):
        block_key = jax.random.fold_in(key, index)
        first_key, second_key, third_key = jax.random.split(block_key, 3)
        raw = jax.random.normal(first_key, (M, M), jnp.float32)
        symmetric = (raw + raw.T) / jnp.sqrt(2.0 * M)
        diagonal = jax.random.uniform(second_key, (M,), jnp.float32, spread_low, spread_high)
        material = jnp.exp(jax.random.uniform(third_key, (), jnp.float32, -1.5, 1.5))
        return ((symmetric + jnp.diag(diagonal)) * material).astype(jnp.bfloat16)
    blocks = lax.map(one_block, jnp.arange(N_ROW * N_COL, dtype=jnp.int32))
    return blocks.reshape(N_ROW, N_COL, M, M)


def draw_flexibility(key, part):
    inner = jax.random.fold_in(key, 11)
    return dominant_blocks(inner, 2.5, 4.0)


def draw_schur(key, part):
    inner = jax.random.fold_in(key, 23)
    return dominant_blocks(inner, 2.5, 4.0)


def draw_coarse_inverse(key, part):
    inner = jax.random.fold_in(key, 37)
    first_key, second_key = jax.random.split(inner)
    raw = jax.random.normal(first_key, (NCO, NCO), jnp.float32)
    symmetric = (raw + raw.T) / jnp.sqrt(2.0 * NCO)
    diagonal = jax.random.uniform(second_key, (NCO,), jnp.float32, 4.0, 8.0)
    return symmetric + jnp.diag(diagonal)


def draw_face_rows(key, part):
    inner = jax.random.fold_in(key, 41)
    first_key, second_key = jax.random.split(inner)
    horizontal = jax.random.randint(first_key, (N_ROW, N_COL - 1), FACE // 8, FACE + 1, jnp.int32)
    horizontal = horizontal.at[0, 0].set(FACE)
    vertical = jax.random.randint(second_key, (N_ROW - 1, N_COL), FACE // 8, FACE + 1, jnp.int32)
    west_side = jnp.pad(horizontal, ((0, 0), (1, 0)))
    east_side = jnp.pad(horizontal, ((0, 0), (0, 1)))
    lower_side = jnp.pad(vertical, ((1, 0), (0, 0)))
    upper_side = jnp.pad(vertical, ((0, 1), (0, 0)))
    return jnp.stack([west_side, east_side, lower_side, upper_side], axis=-1)


def plant(values, own_key, least, high):
    place = [jax.random.randint(jax.random.fold_in(own_key, axis), (), 0, length) for axis, length in enumerate(values.shape)]
    widest = values.shape.index(max(values.shape))
    neighbour = place[:widest] + [(place[widest] + 1) % values.shape[widest]] + place[widest + 1:]
    return values.at[tuple(place)].set(least).at[tuple(neighbour)].set(high)


def steps_of(key, extent, shards, low, high):
    level = 1.0
    for dim, parts in shards:
        steps = jax.random.uniform(jax.random.fold_in(jax.random.fold_in(key, 6), dim), (parts,), jnp.float32, low / len(shards), high / len(shards))
        level = level * jnp.repeat(jnp.exp(steps), extent[dim] // parts).reshape((-1,) + (1,) * (len(extent) - 1 - dim))
    return level


def bell_draw(rng, extent, scale, most, pieces=(), kind=jnp.bfloat16):
    entries = jax.random.normal(rng, extent, jnp.float32) * scale
    if len(pieces) > 0:
        entries = steps_of(rng, extent, pieces, -0.22, 0.18) * entries
    return jnp.clip(entries, min=-most, max=most).astype(kind)


def setup_inputs(seed: int = 0) -> dict:
    key_of = jax.random.split(jax.random.key(seed), 9)
    slip_load = bell_draw(key_of[0], (N_ROW, N_COL, M, R), 1.0, 6.0, ((0, 4), (1, 8)))
    flexibility = draw_flexibility(jax.random.fold_in(key_of[8], 71), 0)
    schur = draw_schur(jax.random.fold_in(key_of[8], 71), 0)
    corner_coupling = bell_draw(key_of[3], (N_ROW, N_COL, NC, M), M ** -0.5, 0.1875, ((0, 4), (1, 8)), jnp.float32)
    coarse_inverse = draw_coarse_inverse(jax.random.fold_in(key_of[8], 71), 0)
    bounds_table = jnp.clip(jnp.exp(jax.random.uniform(key_of[5], (LEVELS,), jnp.float32, math.log(0.3), math.log(3.0))), 0.3, 3.0)
    bound_index = plant(jax.random.randint(key_of[6], (N_ROW, N_COL, M), 0, LEVELS), jax.random.fold_in(key_of[6], 1), 0, LEVELS - 1).astype(jnp.int32)
    face_rows = draw_face_rows(jax.random.fold_in(key_of[8], 71), 0)
    return dict(slip_load=slip_load, flexibility=flexibility, schur=schur, corner_coupling=corner_coupling, coarse_inverse=coarse_inverse, bounds_table=bounds_table, bound_index=bound_index, face_rows=face_rows)


def blockwise(matrices, vectors):
    def product(operands):
        return jnp.dot(operands[0], operands[1], preferred_element_type=jnp.float32)
    return lax.map(product, (matrices, vectors))


def reference(slip_load, flexibility, schur, corner_coupling, coarse_inverse, bounds_table, bound_index, face_rows):
    count = N_ROW * N_COL
    flex_flat = flexibility.reshape(count, M, M)
    schur_flat = schur.reshape(count, M, M)
    levels = jnp.arange(LEVELS, dtype=jnp.int32)
    onehot = (bound_index[..., None] == levels).astype(jnp.float32)
    bound = jnp.sum(onehot * bounds_table.astype(jnp.float32), axis=-1)[..., None]
    slots = jnp.arange(FACE, dtype=jnp.int32)
    live = (slots[None, None, None, :] < face_rows[..., None]).astype(jnp.float32).reshape(N_ROW, N_COL, M, 1)
    loads = slip_load.astype(jnp.float32)
    lam = jnp.clip(loads, -bound, bound)
    for iteration in range(ITERS):
        displacement = blockwise(flex_flat, lam.astype(jnp.bfloat16).reshape(count, M, R)).reshape(N_ROW, N_COL, M, R)
        west_face = displacement[:, :, 0:FACE]
        east_face = displacement[:, :, FACE:2 * FACE]
        lower_face = displacement[:, :, 2 * FACE:3 * FACE]
        upper_face = displacement[:, :, 3 * FACE:]
        nb_west = jnp.pad(east_face[:, :-1], ((0, 0), (1, 0), (0, 0), (0, 0)))
        nb_east = jnp.pad(west_face[:, 1:], ((0, 0), (0, 1), (0, 0), (0, 0)))
        nb_lower = jnp.pad(upper_face[:-1], ((1, 0), (0, 0), (0, 0), (0, 0)))
        nb_upper = jnp.pad(lower_face[1:], ((0, 1), (0, 0), (0, 0), (0, 0)))
        paired = jnp.concatenate([nb_west, nb_east, nb_lower, nb_upper], axis=2)
        jump = live * (displacement - paired - loads)
        corner_force = jnp.einsum('rcki,rcin->rckn', corner_coupling.astype(jnp.float32), jump, precision=lax.Precision.HIGHEST)
        ordered = jnp.transpose(corner_force, (1, 0, 2, 3)).reshape(N_COL * N_ROW * NC, R)
        solved = jnp.dot(coarse_inverse.astype(jnp.float32), ordered, precision=lax.Precision.HIGHEST)
        coarse = jnp.transpose(solved.reshape(N_COL, N_ROW, NC, R), (1, 0, 2, 3))
        projected = jump - jnp.einsum('rcki,rckn->rcin', corner_coupling.astype(jnp.float32), coarse, precision=lax.Precision.HIGHEST)
        projected_b = projected.astype(jnp.bfloat16)
        search = blockwise(schur_flat, projected_b.reshape(count, M, R)).reshape(N_ROW, N_COL, M, R)
        search_b = search.astype(jnp.bfloat16)
        curved = blockwise(flex_flat, search_b.reshape(count, M, R)).reshape(N_ROW, N_COL, M, R)
        gain = jnp.sum(projected_b.astype(jnp.float32) * search, axis=(0, 1, 2))
        curvature = jnp.sum(search_b.astype(jnp.float32) * curved, axis=(0, 1, 2))
        lam = jnp.clip(lam - (gain / curvature)[None, None, None, :] * search, -bound, bound)
    return lam.astype(jnp.bfloat16)
```

```python
import jax
import jax.numpy as jnp
from jax import lax
from jax.sharding import PartitionSpec as P

ITERS = 2
ALL = ("row", "col")
HIGH = lax.Precision.HIGHEST


def passed_round(x, axis, by):
    count = lax.axis_size(axis)
    return lax.ppermute(x, axis, [(i, (i + by) % count) for i in range(count)])


def shared(x):
    count = lax.axis_size(ALL)
    copies = jnp.broadcast_to(x[None], (count, *x.shape))
    return lax.all_to_all(copies, ALL, 0, 0, tiled=True)


def local(
    slip_load,
    flexibility,
    schur,
    corner_coupling,
    coarse_inverse,
    bounds_table,
    bound_index,
    face_rows,
):
    loads = slip_load[0, 0].astype(jnp.float32)
    flex_block = flexibility[0, 0]
    schur_block = schur[0, 0]
    coupling = corner_coupling[0, 0]
    row_count = flex_block.shape[0]
    face_size = row_count // 4
    corners = coupling.shape[0]
    rows, cols = lax.axis_size("row"), lax.axis_size("col")
    padded = -(-corners // 8) * 8
    levels = jnp.arange(bounds_table.shape[0], dtype=jnp.int32)
    onehot = (bound_index[0, 0][:, None] == levels[None, :]).astype(jnp.float32)
    bound = jnp.sum(onehot * bounds_table[None, :], axis=1)[:, None]
    slots = jnp.arange(face_size, dtype=jnp.int32)
    live = (slots[None, :] < face_rows[0, 0][:, None]).astype(jnp.float32).reshape(row_count, 1)

    mine = lax.all_to_all(coarse_inverse.T, "row", 0, 1, tiled=True)
    mine = mine.reshape(corners, cols, rows, corners).transpose(0, 2, 1, 3)
    mine = jnp.pad(mine, ((0, 0), (0, 0), (0, 0), (0, padded - corners)))
    mine = mine.reshape(corners, rows * cols * padded)

    lam = jnp.clip(loads, -bound, bound)
    for iteration in range(ITERS):
        displacement = jnp.dot(
            flex_block, lam.astype(jnp.bfloat16), preferred_element_type=jnp.float32
        )
        faces = displacement.reshape(4, face_size, -1)
        nb_lower = passed_round(faces[3], "row", 1)
        nb_upper = passed_round(faces[2], "row", -1)
        nb_west = passed_round(faces[1], "col", 1)
        nb_east = passed_round(faces[0], "col", -1)
        paired = jnp.concatenate([nb_west, nb_east, nb_lower, nb_upper], axis=0)
        jump = live * (displacement - paired - loads)
        corner_force = jnp.dot(coupling, jump, precision=HIGH)
        forces = shared(jnp.pad(corner_force, ((0, padded - corners), (0, 0))))
        coarse = jnp.dot(mine, forces.reshape(-1, forces.shape[-1]), precision=HIGH)
        correction = lax.dot_general(
            coupling, coarse, (((0,), (0,)), ((), ())), precision=HIGH
        )
        projected = jump - correction
        projected_b = projected.astype(jnp.bfloat16)
        search = jnp.dot(schur_block, projected_b, preferred_element_type=jnp.float32)
        gain = jnp.sum(projected_b.astype(jnp.float32) * search, axis=0)
        search_b = search.astype(jnp.bfloat16)
        curved = jnp.dot(flex_block, search_b, preferred_element_type=jnp.float32)
        curvature = jnp.sum(search_b.astype(jnp.float32) * curved, axis=0)
        sums = jnp.sum(shared(jnp.stack([gain, curvature])), axis=0)
        lam = jnp.clip(lam - (sums[0] / sums[1])[None, :] * search, -bound, bound)
    return lam.astype(jnp.bfloat16)[None, None]


def solution(mesh):
    return jax.shard_map(
        local,
        mesh=mesh,
        in_specs=(
            P("row", "col", None, None),
            P("row", "col", None, None),
            P("row", "col", None, None),
            P("row", "col", None, None),
            P("row", "col"),
            P(),
            P("row", "col", None),
            P("row", "col", None),
        ),
        out_specs=P("row", "col", None, None),
        check_vma=False,
    )
```

```python
import functools

import jax
import jax.numpy as jnp
from jax import lax
from jax.experimental import pallas as pl
from jax.experimental.pallas import tpu as pltpu
from jax.sharding import PartitionSpec as P


ITERS = 2
ALL = ("row", "col")
F32 = jnp.float32
BF16 = jnp.bfloat16
VMEM = pl.BlockSpec(memory_space=pltpu.VMEM)
HBM = pl.BlockSpec(memory_space=pltpu.HBM)


def kernel_call(body, specs, outs, flops, scratch=()):
    return pl.pallas_call(
        body,
        in_specs=specs,
        out_specs=[VMEM] * len(outs),
        out_shape=[jax.ShapeDtypeStruct(shape, dtype) for shape, dtype in outs],
        compiler_params=pltpu.CompilerParams(vmem_limit_bytes=16 << 20),
        cost_estimate=pl.CostEstimate(flops=flops, bytes_accessed=4 << 20, transcendentals=0),
        scratch_shapes=scratch,
    )


def passed_round(x, axis, by):
    count = lax.axis_size(axis)
    return lax.ppermute(x, axis, [(i, (i + by) % count) for i in range(count)])


def from_sides(west, east, lower, upper):
    return [
        passed_round(east, "col", 1),
        passed_round(west, "col", -1),
        passed_round(upper, "row", 1),
        passed_round(lower, "row", -1),
    ]


def in_hbm(x):
    return pltpu.with_memory_space_constraint(x, pltpu.HBM)


def halves(x):
    high = x.astype(BF16)
    return high, (x - high.astype(F32)).astype(BF16)


def fine_dot(a, b):
    a_high, a_low = halves(a)
    b_high, b_low = halves(b)
    both = jnp.concatenate([a_high, a_low], axis=0)
    out = jnp.dot(both, b_high, preferred_element_type=F32)
    rows = a.shape[0]
    return out[:rows] + out[rows:] + jnp.dot(a_high, b_low, preferred_element_type=F32)


def put_faces(flex_ref, lam, face_refs):
    displacement = jnp.dot(flex_ref[...], lam.astype(BF16), preferred_element_type=F32)
    size = face_refs[0].shape[0]
    for f, ref in enumerate(face_refs):
        ref[...] = displacement[f * size : (f + 1) * size]


def begin(levels, table_hbm, index_hbm, live_hbm, loads_hbm, block_hbm, coupling_hbm, *refs):
    flex_hbm, bound_ref, limit_ref, weights_ref, flex_ref = refs[:5]
    face_refs, own_refs = refs[5:9], refs[9:-7]
    table_ref, index_ref, live_ref, loads_ref, block_ref, coupling_ref, sems = refs[-7:]
    size = face_refs[0].shape[0]
    pairs = [
        (table_hbm, table_ref),
        (index_hbm, index_ref),
        (loads_hbm, loads_ref),
        (live_hbm, live_ref),
        (block_hbm, block_ref),
        (coupling_hbm, coupling_ref),
    ]
    slabs = [pl.ds(f * size, size) for f in range(4)]
    pairs += [(flex_hbm.at[slab], flex_ref.at[slab]) for slab in slabs]
    copies = [
        pltpu.make_async_copy(source, target, sems.at[i])
        for i, (source, target) in enumerate(pairs)
    ]
    for copy in copies:
        copy.start()
    for copy in copies[:3]:
        copy.wait()
    index = index_ref[...]
    row = jnp.zeros(index.shape, F32)
    for level in range(levels):
        row = jnp.where(index == level, table_ref[level], row)
    bound = jnp.transpose(jnp.broadcast_to(row, (loads_ref.shape[1], row.shape[1])))
    bound_ref[...] = bound
    lam = jnp.clip(loads_ref[...].astype(F32), -bound, bound).astype(BF16)
    for copy in copies[3:6]:
        copy.wait()
    for f in range(4):
        limit_ref[f : f + 1, :] = jnp.full((1, limit_ref.shape[1]), live_ref[0, f], jnp.int32)
    own(block_ref, *own_refs)
    corners, _, length = coupling_ref.shape
    padded = weights_ref.shape[0] // 3
    coupling = coupling_ref[...].reshape(corners, length)
    if padded > corners:
        rest = jnp.zeros((padded - corners, length), F32)
        coupling = jnp.concatenate([coupling, rest], axis=0)
    high, low = halves(coupling)
    weights_ref[...] = jnp.concatenate([high, low, high], axis=0)
    for f, ref in enumerate(face_refs):
        copies[6 + f].wait()
        ref[...] = jnp.dot(flex_ref[slabs[f], :], lam, preferred_element_type=F32)


def stepped(sums_ref, lam, search_ref, bound):
    sums = jnp.sum(sums_ref[...], axis=0)
    return jnp.clip(lam - (sums[0:1] / sums[1:2]) * search_ref[...], -bound, bound)


def again(sums_ref, loads_ref, search_ref, bound_ref, flex_ref, lam_ref, *face_refs):
    bound = bound_ref[...]
    lam = jnp.clip(loads_ref[...].astype(F32), -bound, bound)
    lam = stepped(sums_ref, lam, search_ref, bound)
    lam_ref[...] = lam
    put_faces(flex_ref, lam, face_refs)


def end(sums_ref, lam_ref, search_ref, bound_ref, out_ref):
    out_ref[...] = stepped(sums_ref, lam_ref[...], search_ref, bound_ref[...]).astype(BF16)


def own(block_ref, *own_refs):
    rows = len(own_refs)
    corners = block_ref.shape[0] // rows
    parts = [block_ref[r * corners : (r + 1) * corners, :] for r in range(rows)]
    for k, ref in enumerate(own_refs):
        up = lax.rem(lax.axis_index("row") + k, rows)
        chosen = parts[0]
        for r in range(1, rows):
            chosen = jnp.where(up == r, parts[r], chosen)
        ref[...] = jnp.zeros(ref.shape, F32)
        ref[0:corners, 0 : chosen.shape[1]] = chosen


def jumps(limit_ref, loads_ref, weights_ref, *refs):
    faces, paired, (jump_ref, force_ref) = refs[:4], refs[4:8], refs[8:]
    size = faces[0].shape[0]
    slot = lax.broadcasted_iota(jnp.int32, faces[0].shape, 0)
    parts = []
    for f in range(4):
        at = slice(f * size, (f + 1) * size)
        part = faces[f][...] - paired[f][...] - loads_ref[at].astype(F32)
        parts.append(jnp.where(slot < limit_ref[f : f + 1, :], part, 0.0))
    jump = jnp.concatenate(parts, axis=0)
    jump_ref[...] = jump
    _, groups, group, width = force_ref.shape
    padded = weights_ref.shape[0] // 3
    high, low = halves(jump)
    force = jnp.dot(weights_ref[0 : 2 * padded, :], high, preferred_element_type=F32)
    force = force[:padded] + force[padded:]
    force += jnp.dot(weights_ref[0:padded, :], low, preferred_element_type=F32)
    force = force[: groups * group].reshape(1, groups, group, width)
    force_ref[...] = jnp.broadcast_to(force, force_ref.shape)


def directions(
    blocks, forces_ref, weights_ref, jump_ref, schur_ref, flex_ref, *refs
):
    mine_refs, (search_ref, sums_ref, ordered_ref) = refs[:blocks], refs[blocks:]
    count, groups, group, width = forces_ref.shape
    rows = blocks
    padded, lanes = mine_refs[0].shape
    corners = groups * group
    span = count * corners // blocks
    cols = count // rows
    if lanes > span:
        for b in range(blocks):
            ordered_ref[b, span:, :] = jnp.zeros((lanes - span, width), F32)
    for r in range(rows):
        for c in range(cols):
            start = (c * rows + r) * corners
            for g in range(groups):
                at = start % span + g * group
                ordered_ref[start // span, at : at + group, :] = forces_ref[r * cols + c, g]
    coarse = jnp.zeros((padded, width), F32)
    for k, mine_ref in enumerate(mine_refs):
        coarse += fine_dot(mine_ref[...], ordered_ref[lax.rem(lax.axis_index("row") + rows - k, rows)])
    high, low = halves(coarse)
    correction = lax.dot_general(
        weights_ref[...],
        jnp.concatenate([high, high, low], axis=0),
        (((0,), (0,)), ((), ())),
        preferred_element_type=F32,
    )
    projected = (jump_ref[...] - correction).astype(BF16)
    search = jnp.dot(schur_ref[...], projected, preferred_element_type=F32)
    search_ref[...] = search
    gain = jnp.sum(projected.astype(F32) * search, axis=0, keepdims=True)
    search = search.astype(BF16)
    curved = jnp.dot(flex_ref[...], search, preferred_element_type=F32)
    curvature = jnp.sum(search.astype(F32) * curved, axis=0, keepdims=True)
    sums = jnp.concatenate([gain, curvature], axis=0)
    sums_ref[...] = jnp.broadcast_to(sums[None], sums_ref.shape)


def local(
    slip_load,
    flexibility,
    schur,
    corner_coupling,
    coarse_inverse,
    bounds_table,
    bound_index,
    face_rows,
):
    loads = slip_load[0, 0]
    flex = flexibility[0, 0]
    shell = schur[0, 0]
    coupling = corner_coupling[0, 0][:, None, :]
    row_count, width = loads.shape
    face = ((row_count // 4, width), F32)
    whole = ((row_count, width), F32)
    rows, cols = lax.axis_size("row"), lax.axis_size("col")
    count = rows * cols
    corners = coupling.shape[0]
    group = 4 if corners % 4 == 0 else 1
    shared = ((count, corners // group, group, width), F32)
    padded = -(-corners // 8) * 8
    lanes = -(-coarse_inverse.shape[0] // 128) * 128
    work = 2 * row_count * row_count * width

    def exchanged(blocks):
        return lax.all_to_all(blocks, ALL, 0, 0, tiled=True)

    inputs = (bounds_table, bound_index[0], face_rows[0], loads, coarse_inverse.T, coupling, flex)
    outs = kernel_call(
        functools.partial(begin, bounds_table.shape[0]),
        [HBM] * 7,
        [
            whole,
            ((8, width), jnp.int32),
            ((3 * padded, row_count), BF16),
            (flex.shape, BF16),
        ]
        + [face] * 4
        + [((padded, lanes), F32)] * rows,
        work,
        [
            pltpu.SMEM(bounds_table.shape, F32),
            pltpu.VMEM((1, row_count), jnp.int32),
            pltpu.SMEM((1, 4), jnp.int32),
            pltpu.VMEM(loads.shape, BF16),
            pltpu.VMEM(coarse_inverse.T.shape, F32),
            pltpu.VMEM(coupling.shape, F32),
            pltpu.SemaphoreType.DMA((10,)),
        ],
    )(*(in_hbm(x) for x in inputs))
    bound, limit, weights, flex = outs[:4]
    faces, mine = outs[4:8], outs[8:]
    for iteration in range(ITERS):
        paired = from_sides(*faces)
        if iteration == 0:
            mine = [mine[0]] + [
                passed_round(block, "row", k) for k, block in enumerate(mine[1:], 1)
            ]
            paired[0], *mine = lax.optimization_barrier((paired[0], *mine))
        jump, forces = kernel_call(
            jumps, [VMEM] * 11, [whole, shared], work // 8
        )(limit, loads, weights, *faces, *paired)
        forces = exchanged(forces)
        search, sums = kernel_call(
            functools.partial(directions, rows),
            [VMEM] * (5 + rows),
            [whole, ((count, 2, width), F32)],
            2 * work,
            [pltpu.VMEM((rows, lanes, width), F32)],
        )(forces, weights, jump, shell, flex, *mine)
        sums = exchanged(sums)
        if iteration < ITERS - 1:
            lam, *faces = kernel_call(
                again, [VMEM] * 5, [whole] + [face] * 4, work
            )(sums, loads, search, bound, flex)
        else:
            (out,) = kernel_call(
                end, [VMEM] * 4, [((row_count, width), BF16)], work // 64
            )(sums, lam, search, bound)
    return out[None, None]


def solution(mesh):
    return jax.shard_map(
        local,
        mesh=mesh,
        in_specs=(
            P("row", "col", None, None),
            P("row", "col", None, None),
            P("row", "col", None, None),
            P("row", "col", None, None),
            P("row", "col"),
            P(),
            P("row", "col", None),
            P("row", "col", None),
        ),
        out_specs=P("row", "col", None, None),
        check_vma=False,
    )
```

```python
import functools

import jax
import jax.numpy as jnp
from jax import lax
from jax.experimental import pallas as pl
from jax.experimental.pallas import tpu as pltpu
from jax.sharding import PartitionSpec as P


ITERS = 2
ALL = ("row", "col")
F32 = jnp.float32
BF16 = jnp.bfloat16
VMEM = pl.BlockSpec(memory_space=pltpu.VMEM)
HBM = pl.BlockSpec(memory_space=pltpu.HBM)


def kernel_call(body, specs, outs, flops, scratch=()):
    return pl.pallas_call(
        body,
        in_specs=specs,
        out_specs=[VMEM] * len(outs),
        out_shape=[jax.ShapeDtypeStruct(shape, dtype) for shape, dtype in outs],
        compiler_params=pltpu.CompilerParams(vmem_limit_bytes=16 << 20),
        cost_estimate=pl.CostEstimate(flops=flops, bytes_accessed=4 << 20, transcendentals=0),
        scratch_shapes=scratch,
    )


def partner(position, count, k):
    return position ^ k if count & (count - 1) == 0 else (position + k) % count


def passed(x, axis, targets):
    return lax.ppermute(x, axis, list(enumerate(targets)))


def swapped(x, axis, first, ends):
    count = lax.axis_size(axis)
    targets = list(range(count))
    for i in range(first, count - 1, 2):
        targets[i], targets[i + 1] = i + 1, i
    if ends and first == 1 and count % 2 == 0:
        targets[0], targets[-1] = count - 1, 0
    return passed(x, axis, targets)


def across(faces):
    return [
        swapped(faces[0], "row", 0, False),
        swapped(faces[1], "row", 1, False),
        swapped(faces[2], "col", 1, True),
        swapped(faces[3], "col", 0, True),
    ]


def face_order():
    row, col = lax.rem(lax.axis_index("row"), 2), lax.rem(lax.axis_index("col"), 2)
    return [3 - row, 2 + row, col, 1 - col]


def in_hbm(x):
    return pltpu.with_memory_space_constraint(x, pltpu.HBM)


def halves(x):
    high = x.astype(BF16)
    return high, (x - high.astype(F32)).astype(BF16)


def two_part_dot(parts_ref, high, low):
    rows = parts_ref.shape[0] // 2
    out = jnp.dot(parts_ref[...], high, preferred_element_type=F32)
    return out[:rows] + out[rows:] + jnp.dot(parts_ref[0:rows, :], low, preferred_element_type=F32)


def slab(face, size):
    return pl.ds(pl.multiple_of(face * size, size), size)


def put_faces(flex_ref, lam, face_refs):
    size = face_refs[0].shape[0]
    for face, ref in zip(face_order(), face_refs):
        ref[...] = jnp.dot(flex_ref[slab(face, size), :], lam, preferred_element_type=F32)


def begin(levels, table_hbm, index_hbm, live_hbm, loads_hbm, coupling_hbm, flex_hbm, *refs):
    bound_ref, limit_ref, weights_ref, flex_ref = refs[:4]
    face_refs = refs[4:8]
    table_ref, index_ref, live_ref, loads_ref, coupling_ref, sems = refs[8:]
    size = face_refs[0].shape[0]
    pairs = [
        (table_hbm, table_ref),
        (index_hbm, index_ref),
        (loads_hbm, loads_ref),
        (live_hbm, live_ref),
        (coupling_hbm, coupling_ref),
    ]
    slabs = [pl.ds(f * size, size) for f in (2, 3, 0, 1)]
    pairs += [(flex_hbm.at[part], flex_ref.at[part]) for part in slabs]
    copies = [
        pltpu.make_async_copy(source, target, sems.at[i])
        for i, (source, target) in enumerate(pairs)
    ]
    for copy in copies:
        copy.start()
    for copy in copies[:3]:
        copy.wait()
    index = index_ref[...]
    row = jnp.zeros(index.shape, F32)
    for level in range(levels):
        row = jnp.where(index == level, table_ref[level], row)
    bound = jnp.transpose(jnp.broadcast_to(row, (loads_ref.shape[1], row.shape[1])))
    bound_ref[...] = bound
    lam = jnp.clip(loads_ref[...].astype(F32), -bound, bound).astype(BF16)
    for copy in copies[3:5]:
        copy.wait()
    for k, face in enumerate(face_order()):
        limit_ref[k : k + 1, :] = jnp.full((1, limit_ref.shape[1]), live_ref[0, face], jnp.int32)
    corners, _, length = coupling_ref.shape
    padded = weights_ref.shape[0] // 3
    coupling = coupling_ref[...].reshape(corners, length)
    if padded > corners:
        rest = jnp.zeros((padded - corners, length), F32)
        coupling = jnp.concatenate([coupling, rest], axis=0)
    high, low = halves(coupling)
    weights_ref[...] = jnp.concatenate([high, low, high], axis=0)
    for half in (slice(0, 2), slice(2, 4)):
        for copy in copies[5:][half]:
            copy.wait()
        for face, ref in list(zip(face_order(), face_refs))[half]:
            ref[...] = jnp.dot(flex_ref[slab(face, size), :], lam, preferred_element_type=F32)


def stepped(sums_ref, lam, search_ref, bound):
    sums = jnp.sum(sums_ref[...], axis=0)
    return jnp.clip(lam - (sums[0:1] / sums[1:2]) * search_ref[...], -bound, bound)


def again(sums_ref, loads_ref, search_ref, bound_ref, flex_ref, lam_ref, *face_refs):
    bound = bound_ref[...]
    lam = jnp.clip(loads_ref[...].astype(F32), -bound, bound)
    lam = stepped(sums_ref, lam, search_ref, bound)
    lam_ref[...] = lam
    put_faces(flex_ref, lam.astype(BF16), face_refs)


def end(sums_ref, lam_ref, search_ref, bound_ref, out_ref):
    out_ref[...] = stepped(sums_ref, lam_ref[...], search_ref, bound_ref[...]).astype(BF16)


def own_rows(block_refs, mine_ref):
    rows = len(block_refs)
    corners = block_refs[0].shape[0] // rows
    padded, lanes = mine_ref.shape[0] // 2, mine_ref.shape[1] // rows
    here = lax.axis_index("row")
    mine_ref[...] = jnp.zeros(mine_ref.shape, BF16)
    for k, ref in enumerate(block_refs):
        chosen = ref[0:corners, :]
        for r in range(1, rows):
            chosen = jnp.where(here == r, ref[r * corners : (r + 1) * corners, :], chosen)
        at = slice(k * lanes, k * lanes + chosen.shape[1])
        high, low = halves(chosen)
        mine_ref[0:corners, at] = high
        mine_ref[padded : padded + corners, at] = low


def jumps(blocks, limit_ref, loads_ref, weights_ref, *refs):
    faces, paired, block_refs = refs[:4], refs[4:8], refs[8 : 8 + blocks]
    jump_ref, force_ref, *mine_refs = refs[8 + blocks :]
    if blocks:
        own_rows(block_refs, *mine_refs)
    size = faces[0].shape[0]
    slot = lax.broadcasted_iota(jnp.int32, faces[0].shape, 0)
    for k, face in enumerate(face_order()):
        at = slab(face, size)
        part = faces[k][...] - paired[k][...] - loads_ref[at, :].astype(F32)
        jump_ref[at, :] = jnp.where(slot < limit_ref[k : k + 1, :], part, 0.0)
    jump = jump_ref[...]
    _, groups, group, width = force_ref.shape
    padded = weights_ref.shape[0] // 3
    high, low = halves(jump)
    force = two_part_dot(weights_ref.at[0 : 2 * padded], high, low)
    force = force[: groups * group].reshape(1, groups, group, width)
    force_ref[...] = jnp.broadcast_to(force, force_ref.shape)


def directions(
    blocks, forces_ref, mine_ref, weights_ref, jump_ref, schur_ref, flex_ref, *refs
):
    search_ref, sums_ref, ordered_ref = refs
    count, groups, group, width = forces_ref.shape
    rows = blocks
    lanes = mine_ref.shape[1] // blocks
    corners = groups * group
    span = count * corners // blocks
    cols = count // rows
    if lanes > span:
        for b in range(blocks):
            ordered_ref[b, span:, :] = jnp.zeros((lanes - span, width), F32)
    for r in range(rows):
        for c in range(cols):
            start = (c * rows + r) * corners
            for g in range(groups):
                at = start % span + g * group
                ordered_ref[start // span, at : at + group, :] = forces_ref[r * cols + c, g]
    here = lax.axis_index("row")
    sources = [partner(here, rows, rows - k if rows & (rows - 1) else k) for k in range(rows)]
    high, low = halves(jnp.concatenate([ordered_ref[source] for source in sources], axis=0))
    coarse = two_part_dot(mine_ref, high, low)
    high, low = halves(coarse)
    correction = lax.dot_general(
        weights_ref[...],
        jnp.concatenate([high, high, low], axis=0),
        (((0,), (0,)), ((), ())),
        preferred_element_type=F32,
    )
    projected = (jump_ref[...] - correction).astype(BF16)
    search = jnp.dot(schur_ref[...], projected, preferred_element_type=F32)
    search_ref[...] = search
    gain = jnp.sum(projected.astype(F32) * search, axis=0, keepdims=True)
    search = search.astype(BF16)
    curved = jnp.dot(flex_ref[...], search, preferred_element_type=F32)
    curvature = jnp.sum(search.astype(F32) * curved, axis=0, keepdims=True)
    sums = jnp.concatenate([gain, curvature], axis=0)
    sums_ref[...] = jnp.broadcast_to(sums[None], sums_ref.shape)


def local(
    slip_load,
    flexibility,
    schur,
    corner_coupling,
    coarse_inverse,
    bounds_table,
    bound_index,
    face_rows,
):
    loads = slip_load[0, 0]
    flex = flexibility[0, 0]
    shell = schur[0, 0]
    coupling = corner_coupling[0, 0][:, None, :]
    row_count, width = loads.shape
    face = ((row_count // 4, width), F32)
    whole = ((row_count, width), F32)
    rows, cols = lax.axis_size("row"), lax.axis_size("col")
    count = rows * cols
    corners = coupling.shape[0]
    group = 4 if corners % 4 == 0 else 1
    shared = ((count, corners // group, group, width), F32)
    padded = -(-corners // 8) * 8
    lanes = -(-coarse_inverse.shape[0] // 128) * 128
    work = 2 * row_count * row_count * width

    def exchanged(blocks):
        return lax.all_to_all(blocks, ALL, 0, 0, tiled=True)

    block = coarse_inverse.T
    blocks = [block] + [
        passed(block, "row", [partner(r, rows, k) for r in range(rows)])
        for k in range(1, rows)
    ]
    inputs = (
        bounds_table,
        bound_index[0],
        face_rows[0],
        loads,
        coupling,
        flex,
    )
    outs = kernel_call(
        functools.partial(begin, bounds_table.shape[0]),
        [HBM] * 6,
        [
            whole,
            ((8, width), jnp.int32),
            ((3 * padded, row_count), BF16),
            (flex.shape, BF16),
        ]
        + [face] * 4,
        work,
        [
            pltpu.SMEM(bounds_table.shape, F32),
            pltpu.VMEM((1, row_count), jnp.int32),
            pltpu.SMEM((1, 4), jnp.int32),
            pltpu.VMEM(loads.shape, BF16),
            pltpu.VMEM(coupling.shape, F32),
            pltpu.SemaphoreType.DMA((9,)),
        ],
    )(*(in_hbm(x) for x in inputs))
    bound, limit, weights, flex = outs[:4]
    faces = outs[4:]
    for iteration in range(ITERS):
        paired = across(faces)
        if iteration == 0:
            paired[0], *blocks = lax.optimization_barrier((paired[0], *blocks))
            jump, forces, mine = kernel_call(
                functools.partial(jumps, rows),
                [VMEM] * (11 + rows),
                [whole, shared, ((2 * padded, rows * lanes), BF16)],
                work // 8,
            )(limit, loads, weights, *faces, *paired, *blocks)
        else:
            jump, forces = kernel_call(
                functools.partial(jumps, 0), [VMEM] * 11, [whole, shared], work // 8
            )(limit, loads, weights, *faces, *paired)
        forces = exchanged(forces)
        search, sums = kernel_call(
            functools.partial(directions, rows),
            [VMEM] * 6,
            [whole, ((count, 2, width), F32)],
            2 * work,
            [pltpu.VMEM((rows, lanes, width), F32)],
        )(forces, mine, weights, jump, shell, flex)
        sums = exchanged(sums)
        if iteration < ITERS - 1:
            lam, *faces = kernel_call(
                again, [VMEM] * 5, [whole] + [face] * 4, work
            )(sums, loads, search, bound, flex)
        else:
            (out,) = kernel_call(
                end, [VMEM] * 4, [((row_count, width), BF16)], work // 64
            )(sums, lam, search, bound)
    return out[None, None]


def solution(mesh):
    return jax.shard_map(
        local,
        mesh=mesh,
        in_specs=(
            P("row", "col", None, None),
            P("row", "col", None, None),
            P("row", "col", None, None),
            P("row", "col", None, None),
            P("row", "col"),
            P(),
            P("row", "col", None),
            P("row", "col", None),
        ),
        out_specs=P("row", "col", None, None),
        check_vma=False,
    )
```

```python
import functools

import jax
import jax.numpy as jnp
from jax import lax
from jax.experimental import pallas as pl
from jax.experimental.pallas import tpu as pltpu
from jax.sharding import PartitionSpec as P


ITERS = 2
ALL = ("row", "col")
F32 = jnp.float32
BF16 = jnp.bfloat16
VMEM = pl.BlockSpec(memory_space=pltpu.VMEM)
HBM = pl.BlockSpec(memory_space=pltpu.HBM)


def kernel_call(body, specs, outs, flops, scratch=()):
    return pl.pallas_call(
        body,
        in_specs=specs,
        out_specs=[VMEM] * len(outs),
        out_shape=[jax.ShapeDtypeStruct(shape, dtype) for shape, dtype in outs],
        compiler_params=pltpu.CompilerParams(vmem_limit_bytes=16 << 20),
        cost_estimate=pl.CostEstimate(flops=flops, bytes_accessed=4 << 20, transcendentals=0),
        scratch_shapes=scratch,
    )


def partner(position, count, k):
    return position ^ k if count & (count - 1) == 0 else (position + k) % count


def passed(x, axis, targets):
    return lax.ppermute(x, axis, list(enumerate(targets)))


def swapped(x, axis, first, ends):
    count = lax.axis_size(axis)
    targets = list(range(count))
    for i in range(first, count - 1, 2):
        targets[i], targets[i + 1] = i + 1, i
    if ends and first == 1 and count % 2 == 0:
        targets[0], targets[-1] = count - 1, 0
    return passed(x, axis, targets)


def across(faces):
    ways = (("row", 0, False), ("row", 1, False), ("col", 1, True), ("col", 0, True))
    out = []
    for k, way in enumerate(ways):
        out.append(swapped(faces[k], *way))
    return out


def face_order():
    row, col = lax.rem(lax.axis_index("row"), 2), lax.rem(lax.axis_index("col"), 2)
    return [3 - row, 2 + row, col, 1 - col]


def in_hbm(x):
    return pltpu.with_memory_space_constraint(x, pltpu.HBM)


def halves(x):
    high = x.astype(BF16)
    return high, (x - high.astype(F32)).astype(BF16)


def two_part_dot(parts_ref, high, low):
    rows = parts_ref.shape[0] // 2
    out = jnp.dot(parts_ref[...], high, preferred_element_type=F32)
    return out[:rows] + out[rows:] + jnp.dot(parts_ref[0:rows, :], low, preferred_element_type=F32)


def slab(face, size):
    return pl.ds(pl.multiple_of(face * size, size), size)


def put_faces(flex_ref, lam, face_refs):
    size = face_refs[0].shape[0]
    for face, ref in zip(face_order(), face_refs):
        ref[...] = jnp.dot(flex_ref[slab(face, size), :], lam, preferred_element_type=F32)


def begin(levels, table_hbm, index_hbm, live_hbm, loads_hbm, coupling_hbm, flex_hbm, *refs):
    bound_ref, limit_ref, weights_ref, flex_ref = refs[:4]
    face_refs = refs[4:8]
    table_ref, index_ref, live_ref, loads_ref, coupling_ref, sems = refs[8:]
    size = face_refs[0].shape[0]
    pairs = [
        (table_hbm, table_ref),
        (index_hbm, index_ref),
        (loads_hbm, loads_ref),
        (live_hbm, live_ref),
        (coupling_hbm, coupling_ref),
    ]
    slabs = [pl.ds(f * size, size) for f in (2, 3, 0, 1)]
    pairs += [(flex_hbm.at[part], flex_ref.at[part]) for part in slabs]
    copies = [
        pltpu.make_async_copy(source, target, sems.at[i])
        for i, (source, target) in enumerate(pairs)
    ]
    for copy in copies:
        copy.start()
    for copy in copies[:3]:
        copy.wait()
    index = index_ref[...]
    row = jnp.zeros(index.shape, F32)
    for level in range(levels):
        row = jnp.where(index == level, table_ref[level], row)
    bound = jnp.transpose(jnp.broadcast_to(row, (loads_ref.shape[1], row.shape[1])))
    bound_ref[...] = bound
    lam = jnp.clip(loads_ref[...].astype(F32), -bound, bound).astype(BF16)
    for copy in copies[3:5]:
        copy.wait()
    for k, face in enumerate(face_order()):
        limit_ref[k : k + 1, :] = jnp.full((1, limit_ref.shape[1]), live_ref[0, face], jnp.int32)
    corners, _, length = coupling_ref.shape
    padded = weights_ref.shape[0] // 3
    coupling = coupling_ref[...].reshape(corners, length)
    if padded > corners:
        rest = jnp.zeros((padded - corners, length), F32)
        coupling = jnp.concatenate([coupling, rest], axis=0)
    high, low = halves(coupling)
    weights_ref[...] = jnp.concatenate([high, low, high], axis=0)
    for half in (slice(0, 2), slice(2, 4)):
        for copy in copies[5:][half]:
            copy.wait()
        for face, ref in list(zip(face_order(), face_refs))[half]:
            ref[...] = jnp.dot(flex_ref[slab(face, size), :], lam, preferred_element_type=F32)


def stepped(sums_ref, lam, search_ref, bound):
    sums = jnp.sum(sums_ref[...], axis=0)
    return jnp.clip(lam - (sums[0:1] / sums[1:2]) * search_ref[...], -bound, bound)


def again(sums_ref, loads_ref, search_ref, bound_ref, flex_ref, lam_ref, *face_refs):
    bound = bound_ref[...]
    lam = jnp.clip(loads_ref[...].astype(F32), -bound, bound)
    lam = stepped(sums_ref, lam, search_ref, bound)
    lam_ref[...] = lam
    put_faces(flex_ref, lam.astype(BF16), face_refs)


def end(sums_ref, lam_ref, search_ref, bound_ref, out_ref):
    out_ref[...] = stepped(sums_ref, lam_ref[...], search_ref, bound_ref[...]).astype(BF16)


def own_rows(block_refs, mine_ref):
    rows = len(block_refs)
    corners = block_refs[0].shape[0] // rows
    padded, lanes = mine_ref.shape[0] // 2, mine_ref.shape[1] // rows
    here = lax.axis_index("row")
    mine_ref[...] = jnp.zeros(mine_ref.shape, BF16)
    for k, ref in enumerate(block_refs):
        chosen = ref[0:corners, :]
        for r in range(1, rows):
            chosen = jnp.where(here == r, ref[r * corners : (r + 1) * corners, :], chosen)
        at = slice(k * lanes, k * lanes + chosen.shape[1])
        high, low = halves(chosen)
        mine_ref[0:corners, at] = high
        mine_ref[padded : padded + corners, at] = low


def jumps(blocks, limit_ref, loads_ref, weights_ref, *refs):
    faces, paired, block_refs = refs[:4], refs[4:8], refs[8 : 8 + blocks]
    jump_ref, force_ref, *mine_refs = refs[8 + blocks :]
    if blocks:
        own_rows(block_refs, *mine_refs)
    size = faces[0].shape[0]
    slot = lax.broadcasted_iota(jnp.int32, faces[0].shape, 0)
    for k, face in enumerate(face_order()):
        at = slab(face, size)
        part = faces[k][...] - paired[k][...] - loads_ref[at, :].astype(F32)
        jump_ref[at, :] = jnp.where(slot < limit_ref[k : k + 1, :], part, 0.0)
    jump = jump_ref[...]
    _, groups, group, width = force_ref.shape
    padded = weights_ref.shape[0] // 3
    high, low = halves(jump)
    force = two_part_dot(weights_ref.at[0 : 2 * padded], high, low)
    force = force[: groups * group].reshape(1, groups, group, width)
    force_ref[...] = jnp.broadcast_to(force, force_ref.shape)


def directions(
    blocks, forces_ref, mine_ref, weights_ref, jump_ref, schur_ref, flex_ref, *refs
):
    search_ref, sums_ref, ordered_ref = refs[:3]
    count, groups, group, width = forces_ref.shape
    rows = blocks
    lanes = mine_ref.shape[1] // blocks
    corners = groups * group
    span = count * corners // blocks
    cols = count // rows
    if lanes > span:
        for b in range(blocks):
            ordered_ref[b, span:, :] = jnp.zeros((lanes - span, width), F32)
    for r in range(rows):
        for c in range(cols):
            start = (c * rows + r) * corners
            for g in range(groups):
                at = start % span + g * group
                ordered_ref[start // span, at : at + group, :] = forces_ref[r * cols + c, g]
    here = lax.axis_index("row")
    sources = [partner(here, rows, rows - k if rows & (rows - 1) else k) for k in range(rows)]
    high, low = halves(jnp.concatenate([ordered_ref[source] for source in sources], axis=0))
    coarse = two_part_dot(mine_ref, high, low)
    high, low = halves(coarse)
    correction = lax.dot_general(
        weights_ref[...],
        jnp.concatenate([high, high, low], axis=0),
        (((0,), (0,)), ((), ())),
        preferred_element_type=F32,
    )
    projected_ref, along_ref = refs[3:]
    projected_ref[...] = (jump_ref[...] - correction).astype(BF16)
    size = jump_ref.shape[0] // 4
    slabs = [slice(at, at + size) for at in range(0, jump_ref.shape[0], size)]
    gain = curvature = jnp.zeros((1, width), F32)
    projected = projected_ref[...]
    for at in slabs:
        search = jnp.dot(schur_ref[at, :], projected, preferred_element_type=F32)
        search_ref[at, :] = search
        along_ref[at, :] = search.astype(BF16)
        gain += jnp.sum(projected_ref[at, :].astype(F32) * search, axis=0, keepdims=True)
    along = along_ref[...]
    for at in slabs:
        curved = jnp.dot(flex_ref[at, :], along, preferred_element_type=F32)
        curvature += jnp.sum(along_ref[at, :].astype(F32) * curved, axis=0, keepdims=True)
    sums = jnp.concatenate([gain, curvature], axis=0)
    sums_ref[...] = jnp.broadcast_to(sums[None], sums_ref.shape)


def local(
    slip_load,
    flexibility,
    schur,
    corner_coupling,
    coarse_inverse,
    bounds_table,
    bound_index,
    face_rows,
):
    loads = slip_load[0, 0]
    flex = flexibility[0, 0]
    shell = schur[0, 0]
    coupling = corner_coupling[0, 0][:, None, :]
    row_count, width = loads.shape
    face = ((row_count // 4, width), F32)
    whole = ((row_count, width), F32)
    rows, cols = lax.axis_size("row"), lax.axis_size("col")
    count = rows * cols
    corners = coupling.shape[0]
    group = 4 if corners % 4 == 0 else 1
    shared = ((count, corners // group, group, width), F32)
    padded = -(-corners // 8) * 8
    lanes = -(-coarse_inverse.shape[0] // 128) * 128
    work = 2 * row_count * row_count * width

    def exchanged(blocks):
        return lax.all_to_all(blocks, ALL, 0, 0, tiled=True)

    block = coarse_inverse.T
    blocks = [block]
    for k in range(1, rows):
        to = [partner(r, rows, k) for r in range(rows)]
        blocks.append(passed(block, "row", to))
    inputs = (
        bounds_table,
        bound_index[0],
        face_rows[0],
        loads,
        coupling,
        flex,
    )
    outs = kernel_call(
        functools.partial(begin, bounds_table.shape[0]),
        [HBM] * 6,
        [
            whole,
            ((8, width), jnp.int32),
            ((3 * padded, row_count), BF16),
            (flex.shape, BF16),
        ]
        + [face] * 4,
        work,
        [
            pltpu.SMEM(bounds_table.shape, F32),
            pltpu.VMEM((1, row_count), jnp.int32),
            pltpu.SMEM((1, 4), jnp.int32),
            pltpu.VMEM(loads.shape, BF16),
            pltpu.VMEM(coupling.shape, F32),
            pltpu.SemaphoreType.DMA((9,)),
        ],
    )(*(in_hbm(x) for x in inputs))
    bound, limit, weights, flex = outs[:4]
    faces = outs[4:]
    for iteration in range(ITERS):
        paired = across(faces)
        if iteration == 0:
            paired[0], *blocks = lax.optimization_barrier((paired[0], *blocks))
            jump, forces, mine = kernel_call(
                functools.partial(jumps, rows),
                [VMEM] * (11 + rows),
                [whole, shared, ((2 * padded, rows * lanes), BF16)],
                work // 8,
            )(limit, loads, weights, *faces, *paired, *blocks)
        else:
            jump, forces = kernel_call(
                functools.partial(jumps, 0), [VMEM] * 11, [whole, shared], work // 8
            )(limit, loads, weights, *faces, *paired)
        forces = exchanged(forces)
        search, sums = kernel_call(
            functools.partial(directions, rows),
            [VMEM] * 6,
            [whole, ((count, 2, width), F32)],
            2 * work,
            [
                pltpu.VMEM((rows, lanes, width), F32),
                pltpu.VMEM((row_count, width), BF16),
                pltpu.VMEM((row_count, width), BF16),
            ],
        )(forces, mine, weights, jump, shell, flex)
        sums = exchanged(sums)
        if iteration < ITERS - 1:
            lam, *faces = kernel_call(
                again, [VMEM] * 5, [whole] + [face] * 4, work
            )(sums, loads, search, bound, flex)
        else:
            (out,) = kernel_call(
                end, [VMEM] * 4, [((row_count, width), BF16)], work // 64
            )(sums, lam, search, bound)
    return out[None, None]


def solution(mesh):
    return jax.shard_map(
        local,
        mesh=mesh,
        in_specs=(
            P("row", "col", None, None),
            P("row", "col", None, None),
            P("row", "col", None, None),
            P("row", "col", None, None),
            P("row", "col"),
            P(),
            P("row", "col", None),
            P("row", "col", None),
        ),
        out_specs=P("row", "col", None, None),
        check_vma=False,
    )
```

```python
import functools

import jax
import jax.numpy as jnp
from jax import lax
from jax.experimental import pallas as pl
from jax.experimental.pallas import tpu as pltpu
from jax.sharding import PartitionSpec as P


ITERS = 2
ALL = ("row", "col")
F32 = jnp.float32
BF16 = jnp.bfloat16
VMEM = pl.BlockSpec(memory_space=pltpu.VMEM)
HBM = pl.BlockSpec(memory_space=pltpu.HBM)


def kernel_call(body, specs, outs, flops, scratch=()):
    return pl.pallas_call(
        body,
        in_specs=specs,
        out_specs=[VMEM] * len(outs),
        out_shape=[jax.ShapeDtypeStruct(shape, dtype) for shape, dtype in outs],
        compiler_params=pltpu.CompilerParams(vmem_limit_bytes=16 << 20),
        cost_estimate=pl.CostEstimate(flops=flops, bytes_accessed=4 << 20, transcendentals=0),
        scratch_shapes=scratch,
    )


def partner(position, count, k):
    return position ^ k if count & (count - 1) == 0 else (position + k) % count


def passed(x, axis, targets):
    return lax.ppermute(x, axis, list(enumerate(targets)))


def swapped(x, axis, first, wrap):
    rows, cols = lax.axis_size("row"), lax.axis_size("col")
    targets = []
    for r in range(rows):
        for c in range(cols):
            count, i = (rows, r) if axis == "row" else (cols, c)
            j = i ^ 1 if first == 0 else ((i + 1) ^ 1) - 1
            if wrap and first == 1 and count % 2 == 0:
                j %= count
            if 0 <= j < count:
                to = (j, c) if axis == "row" else (r, j)
            elif axis == "row":
                to = (r, c ^ 1) if c ^ 1 < cols else (r, c)
            else:
                to = (r ^ 1, c) if r ^ 1 < rows else (r, c)
            targets.append(to[0] * cols + to[1])
    return passed(x, ALL, targets)


def across(faces):
    ways = (("row", 0, False), ("row", 1, False), ("col", 1, True), ("col", 0, True))
    out = []
    for k, way in enumerate(ways):
        out.append(swapped(faces[k], *way))
    return out


def face_order():
    row, col = lax.rem(lax.axis_index("row"), 2), lax.rem(lax.axis_index("col"), 2)
    return [3 - row, 2 + row, col, 1 - col]


def in_hbm(x):
    return pltpu.with_memory_space_constraint(x, pltpu.HBM)


def halves(x):
    high = x.astype(BF16)
    return high, (x - high.astype(F32)).astype(BF16)


def two_part_dot(parts_ref, high, low):
    rows = parts_ref.shape[0] // 2
    out = jnp.dot(parts_ref[...], high, preferred_element_type=F32)
    return out[:rows] + out[rows:] + jnp.dot(parts_ref[0:rows, :], low, preferred_element_type=F32)


def slab(face, size):
    return pl.ds(pl.multiple_of(face * size, size), size)


def put_pair(rows, lam, flipped, refs):
    both = jnp.dot(rows, lam, preferred_element_type=F32)
    size = both.shape[0] // 2
    first, second = both[:size], both[size:]
    refs[0][...] = jnp.where(flipped, second, first)
    refs[1][...] = jnp.where(flipped, first, second)


def put_faces(flex_ref, lam, face_refs):
    size = 2 * face_refs[0].shape[0]
    order = face_order()
    put_pair(flex_ref[size:, :], lam, order[0] == 3, face_refs[:2])
    put_pair(flex_ref[:size, :], lam, order[2] == 1, face_refs[2:])


def begin(levels, table_hbm, index_hbm, live_hbm, loads_hbm, coupling_hbm, flex_hbm, *refs):
    bound_ref, limit_ref, weights_ref, flex_ref = refs[:4]
    face_refs = refs[4:8]
    table_ref, index_ref, live_ref, loads_ref, coupling_ref, sems = refs[8:]
    size = face_refs[0].shape[0]
    pairs = [
        (table_hbm, table_ref),
        (index_hbm, index_ref),
        (loads_hbm, loads_ref),
        (live_hbm, live_ref),
        (coupling_hbm, coupling_ref),
    ]
    slabs = [pl.ds(f * size, size) for f in (2, 3, 0, 1)]
    pairs += [(flex_hbm.at[part], flex_ref.at[part]) for part in slabs]
    copies = [
        pltpu.make_async_copy(source, target, sems.at[i])
        for i, (source, target) in enumerate(pairs)
    ]
    for copy in copies:
        copy.start()
    for copy in copies[:3]:
        copy.wait()
    index = index_ref[...]
    row = jnp.zeros(index.shape, F32)
    for level in range(levels):
        row = jnp.where(index == level, table_ref[level], row)
    bound = jnp.transpose(jnp.broadcast_to(row, (loads_ref.shape[1], row.shape[1])))
    bound_ref[...] = bound
    lam = jnp.clip(loads_ref[...].astype(F32), -bound, bound).astype(BF16)
    for copy in copies[3:5]:
        copy.wait()
    for k, face in enumerate(face_order()):
        limit_ref[k : k + 1, :] = jnp.full((1, limit_ref.shape[1]), live_ref[0, face], jnp.int32)
    corners, _, length = coupling_ref.shape
    padded = weights_ref.shape[0] // 3
    coupling = coupling_ref[...].reshape(corners, length)
    if padded > corners:
        rest = jnp.zeros((padded - corners, length), F32)
        coupling = jnp.concatenate([coupling, rest], axis=0)
    high, low = halves(coupling)
    weights_ref[...] = jnp.concatenate([high, low, high], axis=0)
    for half in (slice(0, 2), slice(2, 4)):
        for copy in copies[5:][half]:
            copy.wait()
        for face, ref in list(zip(face_order(), face_refs))[half]:
            ref[...] = jnp.dot(flex_ref[slab(face, size), :], lam, preferred_element_type=F32)


def stepped(sums_ref, lam, search_ref, bound):
    sums = jnp.sum(sums_ref[...], axis=0)
    return jnp.clip(lam - (sums[0:1] / sums[1:2]) * search_ref[...], -bound, bound)


def again(sums_ref, loads_ref, search_ref, bound_ref, flex_ref, lam_ref, *face_refs):
    bound = bound_ref[...]
    lam = jnp.clip(loads_ref[...].astype(F32), -bound, bound)
    lam = stepped(sums_ref, lam, search_ref, bound)
    lam_ref[...] = lam
    put_faces(flex_ref, lam.astype(BF16), face_refs)


def end(sums_ref, lam_ref, search_ref, bound_ref, out_ref):
    out_ref[...] = stepped(sums_ref, lam_ref[...], search_ref, bound_ref[...]).astype(BF16)


def own_rows(block_refs, mine_ref):
    rows = len(block_refs)
    corners = block_refs[0].shape[0] // rows
    padded, lanes = mine_ref.shape[0] // 2, mine_ref.shape[1] // rows
    here = lax.axis_index("row")
    mine_ref[...] = jnp.zeros(mine_ref.shape, BF16)
    for k, ref in enumerate(block_refs):
        chosen = ref[0:corners, :]
        for r in range(1, rows):
            chosen = jnp.where(here == r, ref[r * corners : (r + 1) * corners, :], chosen)
        at = slice(k * lanes, k * lanes + chosen.shape[1])
        high, low = halves(chosen)
        mine_ref[0:corners, at] = high
        mine_ref[padded : padded + corners, at] = low


def jumps(blocks, limit_ref, loads_ref, weights_ref, *refs):
    faces, paired, block_refs = refs[:4], refs[4:8], refs[8 : 8 + blocks]
    jump_ref, force_ref, *mine_refs = refs[8 + blocks :]
    if blocks:
        own_rows(block_refs, *mine_refs)
    size = faces[0].shape[0]
    slot = lax.broadcasted_iota(jnp.int32, faces[0].shape, 0)
    for k, face in enumerate(face_order()):
        at = slab(face, size)
        part = faces[k][...] - paired[k][...] - loads_ref[at, :].astype(F32)
        jump_ref[at, :] = jnp.where(slot < limit_ref[k : k + 1, :], part, 0.0)
    jump = jump_ref[...]
    _, groups, group, width = force_ref.shape
    padded = weights_ref.shape[0] // 3
    high, low = halves(jump)
    force = two_part_dot(weights_ref.at[0 : 2 * padded], high, low)
    force = force[: groups * group].reshape(1, groups, group, width)
    force_ref[...] = jnp.broadcast_to(force, force_ref.shape)


def directions(
    blocks, forces_ref, mine_ref, weights_ref, jump_ref, schur_ref, flex_ref, *refs
):
    search_ref, sums_ref, ordered_ref = refs[:3]
    count, groups, group, width = forces_ref.shape
    rows = blocks
    lanes = mine_ref.shape[1] // blocks
    corners = groups * group
    span = count * corners // blocks
    cols = count // rows
    if lanes > span:
        for b in range(blocks):
            ordered_ref[b, span:, :] = jnp.zeros((lanes - span, width), F32)
    for r in range(rows):
        for c in range(cols):
            start = (c * rows + r) * corners
            for g in range(groups):
                at = start % span + g * group
                ordered_ref[start // span, at : at + group, :] = forces_ref[r * cols + c, g]
    here = lax.axis_index("row")
    sources = [partner(here, rows, rows - k if rows & (rows - 1) else k) for k in range(rows)]
    high, low = halves(jnp.concatenate([ordered_ref[source] for source in sources], axis=0))
    coarse = two_part_dot(mine_ref, high, low)
    high, low = halves(coarse)
    correction = lax.dot_general(
        weights_ref[...],
        jnp.concatenate([high, high, low], axis=0),
        (((0,), (0,)), ((), ())),
        preferred_element_type=F32,
    )
    projected_ref, along_ref = refs[3:]
    projected_ref[...] = (jump_ref[...] - correction).astype(BF16)
    size = jump_ref.shape[0] // 2
    slabs = [slice(at, at + size) for at in range(0, jump_ref.shape[0], size)]
    gain = curvature = jnp.zeros((1, width), F32)
    projected = projected_ref[...]
    for at in slabs:
        search = jnp.dot(schur_ref[at, :], projected, preferred_element_type=F32)
        search_ref[at, :] = search
        along_ref[at, :] = search.astype(BF16)
        gain += jnp.sum(projected_ref[at, :].astype(F32) * search, axis=0, keepdims=True)
    along = along_ref[...]
    for at in slabs:
        curved = jnp.dot(flex_ref[at, :], along, preferred_element_type=F32)
        curvature += jnp.sum(along_ref[at, :].astype(F32) * curved, axis=0, keepdims=True)
    sums = jnp.concatenate([gain, curvature], axis=0)
    sums_ref[...] = jnp.broadcast_to(sums[None], sums_ref.shape)


def local(
    slip_load,
    flexibility,
    schur,
    corner_coupling,
    coarse_inverse,
    bounds_table,
    bound_index,
    face_rows,
):
    loads = slip_load[0, 0]
    flex = flexibility[0, 0]
    shell = schur[0, 0]
    coupling = corner_coupling[0, 0][:, None, :]
    row_count, width = loads.shape
    face = ((row_count // 4, width), F32)
    whole = ((row_count, width), F32)
    rows, cols = lax.axis_size("row"), lax.axis_size("col")
    count = rows * cols
    corners = coupling.shape[0]
    group = 4 if corners % 4 == 0 else 1
    shared = ((count, corners // group, group, width), F32)
    padded = -(-corners // 8) * 8
    lanes = -(-coarse_inverse.shape[0] // 128) * 128
    work = 2 * row_count * row_count * width

    def exchanged(blocks):
        return lax.all_to_all(blocks, ALL, 0, 0, tiled=True)

    block = coarse_inverse.T
    blocks = [block]
    for k in range(1, rows):
        to = [partner(r, rows, k) for r in range(rows)]
        blocks.append(passed(block, "row", to))
    inputs = (
        bounds_table,
        bound_index[0],
        face_rows[0],
        loads,
        coupling,
        flex,
    )
    outs = kernel_call(
        functools.partial(begin, bounds_table.shape[0]),
        [HBM] * 6,
        [
            whole,
            ((8, width), jnp.int32),
            ((3 * padded, row_count), BF16),
            (flex.shape, BF16),
        ]
        + [face] * 4,
        work,
        [
            pltpu.SMEM(bounds_table.shape, F32),
            pltpu.VMEM((1, row_count), jnp.int32),
            pltpu.SMEM((1, 4), jnp.int32),
            pltpu.VMEM(loads.shape, BF16),
            pltpu.VMEM(coupling.shape, F32),
            pltpu.SemaphoreType.DMA((9,)),
        ],
    )(*(in_hbm(x) for x in inputs))
    bound, limit, weights, flex = outs[:4]
    faces = outs[4:]
    for iteration in range(ITERS):
        paired = across(faces)
        if iteration == 0:
            paired[0], *blocks = lax.optimization_barrier((paired[0], *blocks))
            jump, forces, mine = kernel_call(
                functools.partial(jumps, rows),
                [VMEM] * (11 + rows),
                [whole, shared, ((2 * padded, rows * lanes), BF16)],
                work // 8,
            )(limit, loads, weights, *faces, *paired, *blocks)
        else:
            jump, forces = kernel_call(
                functools.partial(jumps, 0), [VMEM] * 11, [whole, shared], work // 8
            )(limit, loads, weights, *faces, *paired)
        forces = exchanged(forces)
        search, sums = kernel_call(
            functools.partial(directions, rows),
            [VMEM] * 6,
            [whole, ((count, 2, width), F32)],
            2 * work,
            [
                pltpu.VMEM((rows, lanes, width), F32),
                pltpu.VMEM((row_count, width), BF16),
                pltpu.VMEM((row_count, width), BF16),
            ],
        )(forces, mine, weights, jump, shell, flex)
        sums = exchanged(sums)
        if iteration < ITERS - 1:
            lam, *faces = kernel_call(
                again, [VMEM] * 5, [whole] + [face] * 4, work
            )(sums, loads, search, bound, flex)
        else:
            (out,) = kernel_call(
                end, [VMEM] * 4, [((row_count, width), BF16)], work // 64
            )(sums, lam, search, bound)
    return out[None, None]


def solution(mesh):
    return jax.shard_map(
        local,
        mesh=mesh,
        in_specs=(
            P("row", "col", None, None),
            P("row", "col", None, None),
            P("row", "col", None, None),
            P("row", "col", None, None),
            P("row", "col"),
            P(),
            P("row", "col", None),
            P("row", "col", None),
        ),
        out_specs=P("row", "col", None, None),
        check_vma=False,
    )
```

```python
import functools

import jax
import jax.numpy as jnp
from jax import lax
from jax.experimental import pallas as pl
from jax.experimental.pallas import tpu as pltpu
from jax.sharding import PartitionSpec as P


ITERS = 2
ALL = ("row", "col")
F32 = jnp.float32
BF16 = jnp.bfloat16
VMEM = pl.BlockSpec(memory_space=pltpu.VMEM)
HBM = pl.BlockSpec(memory_space=pltpu.HBM)


def kernel_call(body, specs, outs, flops, scratch=()):
    return pl.pallas_call(
        body,
        in_specs=specs,
        out_specs=[VMEM] * len(outs),
        out_shape=[jax.ShapeDtypeStruct(shape, dtype) for shape, dtype in outs],
        compiler_params=pltpu.CompilerParams(vmem_limit_bytes=16 << 20),
        cost_estimate=pl.CostEstimate(flops=flops, bytes_accessed=4 << 20, transcendentals=0),
        scratch_shapes=scratch,
    )


def partner(position, count, k):
    return position ^ k if count & (count - 1) == 0 else (position + k) % count


def passed(x, axis, targets):
    return lax.ppermute(x, axis, list(enumerate(targets)))


def swapped(x, axis, first, wrap):
    rows, cols = lax.axis_size("row"), lax.axis_size("col")
    targets = []
    for r in range(rows):
        for c in range(cols):
            count, i = (rows, r) if axis == "row" else (cols, c)
            j = i ^ 1 if first == 0 else ((i + 1) ^ 1) - 1
            if wrap and first == 1 and count % 2 == 0:
                j %= count
            if 0 <= j < count:
                to = (j, c) if axis == "row" else (r, j)
            elif axis == "row":
                to = (r, c ^ 1) if c ^ 1 < cols else (r, c)
            else:
                to = (r ^ 1, c) if r ^ 1 < rows else (r, c)
            targets.append(to[0] * cols + to[1])
    return passed(x, ALL, targets)


def across(faces):
    ways = (("row", 0, False), ("row", 1, False), ("col", 1, True), ("col", 0, True))
    out = []
    for k, way in enumerate(ways):
        out.append(swapped(faces[k], *way))
    return out


def face_order():
    row, col = lax.rem(lax.axis_index("row"), 2), lax.rem(lax.axis_index("col"), 2)
    return [3 - row, 2 + row, col, 1 - col]


def in_hbm(x):
    return pltpu.with_memory_space_constraint(x, pltpu.HBM)


def halves(x):
    high = x.astype(BF16)
    return high, (x - high.astype(F32)).astype(BF16)


def two_part_dot(parts_ref, high, low):
    rows = parts_ref.shape[0] // 2
    out = jnp.dot(parts_ref[...], high, preferred_element_type=F32)
    return out[:rows] + out[rows:] + jnp.dot(parts_ref[0:rows, :], low, preferred_element_type=F32)


def slab(face, size):
    return pl.ds(pl.multiple_of(face * size, size), size)


def put_faces(flex_ref, lam, face_refs):
    size = face_refs[0].shape[0]
    for face, ref in zip(face_order(), face_refs):
        ref[...] = jnp.dot(flex_ref[slab(face, size), :], lam, preferred_element_type=F32)


def begin(levels, table_hbm, index_hbm, live_hbm, loads_hbm, coupling_hbm, flex_hbm, *refs):
    bound_ref, limit_ref, weights_ref, flex_ref = refs[:4]
    face_refs = refs[4:8]
    table_ref, index_ref, live_ref, loads_ref, coupling_ref, sems = refs[8:]
    size = face_refs[0].shape[0]
    pairs = [
        (table_hbm, table_ref),
        (index_hbm, index_ref),
        (loads_hbm, loads_ref),
        (live_hbm, live_ref),
        (coupling_hbm, coupling_ref),
    ]
    slabs = [pl.ds(2 * size, 2 * size), pl.ds(0, 2 * size)]
    pairs += [(flex_hbm.at[part], flex_ref.at[part]) for part in slabs]
    copies = [
        pltpu.make_async_copy(source, target, sems.at[i])
        for i, (source, target) in enumerate(pairs)
    ]
    for copy in copies:
        copy.start()
    for copy in copies[:3]:
        copy.wait()
    index = index_ref[...]
    row = jnp.zeros(index.shape, F32)
    for level in range(levels):
        row = jnp.where(index == level, table_ref[level], row)
    bound = jnp.transpose(jnp.broadcast_to(row, (loads_ref.shape[1], row.shape[1])))
    bound_ref[...] = bound
    lam = jnp.clip(loads_ref[...].astype(F32), -bound, bound).astype(BF16)
    for copy in copies[3:5]:
        copy.wait()
    for k, face in enumerate(face_order()):
        limit_ref[k : k + 1, :] = jnp.full((1, limit_ref.shape[1]), live_ref[0, face], jnp.int32)
    corners, _, length = coupling_ref.shape
    padded = weights_ref.shape[0] // 3
    coupling = coupling_ref[...].reshape(corners, length)
    if padded > corners:
        rest = jnp.zeros((padded - corners, length), F32)
        coupling = jnp.concatenate([coupling, rest], axis=0)
    high, low = halves(coupling)
    weights_ref[...] = jnp.concatenate([high, low, high], axis=0)
    for half in (slice(0, 2), slice(2, 4)):
        copies[5 + half.start // 2].wait()
        for face, ref in list(zip(face_order(), face_refs))[half]:
            ref[...] = jnp.dot(flex_ref[slab(face, size), :], lam, preferred_element_type=F32)


def stepped(sums_ref, lam, search_ref, bound):
    sums = jnp.sum(sums_ref[...], axis=0)
    return jnp.clip(lam - (sums[0:1] / sums[1:2]) * search_ref[...], -bound, bound)


def again(sums_ref, loads_ref, search_ref, bound_ref, flex_ref, lam_ref, *face_refs):
    bound = bound_ref[...]
    lam = jnp.clip(loads_ref[...].astype(F32), -bound, bound)
    lam = stepped(sums_ref, lam, search_ref, bound)
    lam_ref[...] = lam
    put_faces(flex_ref, lam.astype(BF16), face_refs)


def end(sums_ref, lam_ref, search_ref, bound_ref, out_ref):
    out_ref[...] = stepped(sums_ref, lam_ref[...], search_ref, bound_ref[...]).astype(BF16)


def own_rows(block_refs, mine_ref):
    rows = len(block_refs)
    corners = block_refs[0].shape[0] // rows
    padded, lanes = mine_ref.shape[0] // 2, mine_ref.shape[1] // rows
    here = lax.axis_index("row")
    mine_ref[...] = jnp.zeros(mine_ref.shape, BF16)
    for k, ref in enumerate(block_refs):
        chosen = ref[0:corners, :]
        for r in range(1, rows):
            chosen = jnp.where(here == r, ref[r * corners : (r + 1) * corners, :], chosen)
        at = slice(k * lanes, k * lanes + chosen.shape[1])
        high, low = halves(chosen)
        mine_ref[0:corners, at] = high
        mine_ref[padded : padded + corners, at] = low


def jumps(blocks, limit_ref, loads_ref, weights_ref, *refs):
    faces, paired, block_refs = refs[:4], refs[4:8], refs[8 : 8 + blocks]
    jump_ref, force_ref, *mine_refs = refs[8 + blocks :]
    if blocks:
        own_rows(block_refs, *mine_refs)
    size = faces[0].shape[0]
    slot = lax.broadcasted_iota(jnp.int32, faces[0].shape, 0)
    for k, face in enumerate(face_order()):
        at = slab(face, size)
        part = faces[k][...] - paired[k][...] - loads_ref[at, :].astype(F32)
        jump_ref[at, :] = jnp.where(slot < limit_ref[k : k + 1, :], part, 0.0)
    jump = jump_ref[...]
    _, groups, group, width = force_ref.shape
    padded = weights_ref.shape[0] // 3
    high, low = halves(jump)
    force = two_part_dot(weights_ref.at[0 : 2 * padded], high, low)
    force = force[: groups * group].reshape(1, groups, group, width)
    force_ref[...] = jnp.broadcast_to(force, force_ref.shape)


def directions(
    blocks, forces_ref, mine_ref, weights_ref, jump_ref, schur_ref, flex_ref, *refs
):
    search_ref, sums_ref, ordered_ref = refs[:3]
    count, groups, group, width = forces_ref.shape
    rows = blocks
    lanes = mine_ref.shape[1] // blocks
    corners = groups * group
    span = count * corners // blocks
    cols = count // rows
    if lanes > span:
        for b in range(blocks):
            ordered_ref[b, span:, :] = jnp.zeros((lanes - span, width), F32)
    for r in range(rows):
        for c in range(cols):
            start = (c * rows + r) * corners
            for g in range(groups):
                at = start % span + g * group
                ordered_ref[start // span, at : at + group, :] = forces_ref[r * cols + c, g]
    here = lax.axis_index("row")
    sources = [partner(here, rows, rows - k if rows & (rows - 1) else k) for k in range(rows)]
    high, low = halves(jnp.concatenate([ordered_ref[source] for source in sources], axis=0))
    coarse = two_part_dot(mine_ref, high, low)
    high, low = halves(coarse)
    correction = lax.dot_general(
        weights_ref[...],
        jnp.concatenate([high, high, low], axis=0),
        (((0,), (0,)), ((), ())),
        preferred_element_type=F32,
    )
    projected_ref, along_ref = refs[3:]
    projected_ref[...] = (jump_ref[...] - correction).astype(BF16)
    size = jump_ref.shape[0] // 4
    slabs = [slice(at, at + size) for at in range(0, jump_ref.shape[0], size)]
    gain = curvature = jnp.zeros((1, width), F32)
    projected = projected_ref[...]
    for at in slabs:
        search = jnp.dot(schur_ref[at, :], projected, preferred_element_type=F32)
        search_ref[at, :] = search
        along_ref[at, :] = search.astype(BF16)
        gain += jnp.sum(projected_ref[at, :].astype(F32) * search, axis=0, keepdims=True)
    along = along_ref[...]
    for at in slabs:
        curved = jnp.dot(flex_ref[at, :], along, preferred_element_type=F32)
        curvature += jnp.sum(along_ref[at, :].astype(F32) * curved, axis=0, keepdims=True)
    sums = jnp.concatenate([gain, curvature], axis=0)
    sums_ref[...] = jnp.broadcast_to(sums[None], sums_ref.shape)


def local(
    slip_load,
    flexibility,
    schur,
    corner_coupling,
    coarse_inverse,
    bounds_table,
    bound_index,
    face_rows,
):
    loads = slip_load[0, 0]
    flex = flexibility[0, 0]
    shell = schur[0, 0]
    coupling = corner_coupling[0, 0][:, None, :]
    row_count, width = loads.shape
    face = ((row_count // 4, width), F32)
    whole = ((row_count, width), F32)
    rows, cols = lax.axis_size("row"), lax.axis_size("col")
    count = rows * cols
    corners = coupling.shape[0]
    group = 4 if corners % 4 == 0 else 1
    shared = ((count, corners // group, group, width), F32)
    padded = -(-corners // 8) * 8
    lanes = -(-coarse_inverse.shape[0] // 128) * 128
    work = 2 * row_count * row_count * width

    def exchanged(blocks):
        return lax.all_to_all(blocks, ALL, 0, 0, tiled=True)

    block = coarse_inverse.T
    blocks = [block]
    for k in range(1, rows):
        to = [partner(r, rows, k) for r in range(rows)]
        blocks.append(passed(block, "row", to))
    inputs = (
        bounds_table,
        bound_index[0],
        face_rows[0],
        loads,
        coupling,
        flex,
    )
    outs = kernel_call(
        functools.partial(begin, bounds_table.shape[0]),
        [HBM] * 6,
        [
            whole,
            ((8, width), jnp.int32),
            ((3 * padded, row_count), BF16),
            (flex.shape, BF16),
        ]
        + [face] * 4,
        work,
        [
            pltpu.SMEM(bounds_table.shape, F32),
            pltpu.VMEM((1, row_count), jnp.int32),
            pltpu.SMEM((1, 4), jnp.int32),
            pltpu.VMEM(loads.shape, BF16),
            pltpu.VMEM(coupling.shape, F32),
            pltpu.SemaphoreType.DMA((7,)),
        ],
    )(*(in_hbm(x) for x in inputs))
    bound, limit, weights, flex = outs[:4]
    faces = outs[4:]
    for iteration in range(ITERS):
        paired = across(faces)
        if iteration == 0:
            paired[0], *blocks = lax.optimization_barrier((paired[0], *blocks))
            jump, forces, mine = kernel_call(
                functools.partial(jumps, rows),
                [VMEM] * (11 + rows),
                [whole, shared, ((2 * padded, rows * lanes), BF16)],
                work // 8,
            )(limit, loads, weights, *faces, *paired, *blocks)
        else:
            jump, forces = kernel_call(
                functools.partial(jumps, 0), [VMEM] * 11, [whole, shared], work // 8
            )(limit, loads, weights, *faces, *paired)
        forces = exchanged(forces)
        search, sums = kernel_call(
            functools.partial(directions, rows),
            [VMEM] * 6,
            [whole, ((count, 2, width), F32)],
            2 * work,
            [
                pltpu.VMEM((rows, lanes, width), F32),
                pltpu.VMEM((row_count, width), BF16),
                pltpu.VMEM((row_count, width), BF16),
            ],
        )(forces, mine, weights, jump, shell, flex)
        sums = exchanged(sums)
        if iteration < ITERS - 1:
            lam, *faces = kernel_call(
                again, [VMEM] * 5, [whole] + [face] * 4, work
            )(sums, loads, search, bound, flex)
        else:
            (out,) = kernel_call(
                end, [VMEM] * 4, [((row_count, width), BF16)], work // 64
            )(sums, lam, search, bound)
    return out[None, None]


def solution(mesh):
    return jax.shard_map(
        local,
        mesh=mesh,
        in_specs=(
            P("row", "col", None, None),
            P("row", "col", None, None),
            P("row", "col", None, None),
            P("row", "col", None, None),
            P("row", "col"),
            P(),
            P("row", "col", None),
            P("row", "col", None),
        ),
        out_specs=P("row", "col", None, None),
        check_vma=False,
    )
```

```python
import functools

import jax
import jax.numpy as jnp
from jax import lax
from jax.experimental import pallas as pl
from jax.experimental.pallas import tpu as pltpu
from jax.sharding import PartitionSpec as P


ITERS = 2
ALL = ("row", "col")
F32 = jnp.float32
BF16 = jnp.bfloat16
VMEM = pl.BlockSpec(memory_space=pltpu.VMEM)
HBM = pl.BlockSpec(memory_space=pltpu.HBM)


def kernel_call(body, specs, outs, flops, scratch=()):
    return pl.pallas_call(
        body,
        in_specs=specs,
        out_specs=[VMEM] * len(outs),
        out_shape=[jax.ShapeDtypeStruct(shape, dtype) for shape, dtype in outs],
        compiler_params=pltpu.CompilerParams(vmem_limit_bytes=16 << 20),
        cost_estimate=pl.CostEstimate(flops=flops, bytes_accessed=4 << 20, transcendentals=0),
        scratch_shapes=scratch,
    )


def partner(position, count, k):
    return position ^ k if count & (count - 1) == 0 else (position + k) % count


def passed(x, axis, targets):
    return lax.ppermute(x, axis, list(enumerate(targets)))


def swapped(x, axis, first, wrap):
    rows, cols = lax.axis_size("row"), lax.axis_size("col")
    targets = []
    for r in range(rows):
        for c in range(cols):
            count, i = (rows, r) if axis == "row" else (cols, c)
            j = i ^ 1 if first == 0 else ((i + 1) ^ 1) - 1
            if wrap and first == 1 and count % 2 == 0:
                j %= count
            if 0 <= j < count:
                to = (j, c) if axis == "row" else (r, j)
            elif axis == "row":
                to = (r, c ^ 1) if c ^ 1 < cols else (r, c)
            else:
                to = (r ^ 1, c) if r ^ 1 < rows else (r, c)
            targets.append(to[0] * cols + to[1])
    return passed(x, ALL, targets)


def across(faces):
    ways = (("row", 0, False), ("row", 1, False), ("col", 1, True), ("col", 0, True))
    out = []
    for k, way in enumerate(ways):
        out.append(swapped(faces[k], *way))
    return out


def face_order():
    row, col = lax.rem(lax.axis_index("row"), 2), lax.rem(lax.axis_index("col"), 2)
    return [3 - row, 2 + row, col, 1 - col]


def in_hbm(x):
    return pltpu.with_memory_space_constraint(x, pltpu.HBM)


def halves(x):
    high = x.astype(BF16)
    return high, (x - high.astype(F32)).astype(BF16)


def two_part_dot(parts_ref, high, low):
    rows = parts_ref.shape[0] // 2
    out = jnp.dot(parts_ref[...], high, preferred_element_type=F32)
    return out[:rows] + out[rows:] + jnp.dot(parts_ref[0:rows, :], low, preferred_element_type=F32)


def slab(face, size):
    return pl.ds(pl.multiple_of(face * size, size), size)


def put_faces(flex_ref, lam, face_refs):
    size = face_refs[0].shape[0]
    for face, ref in zip(face_order(), face_refs):
        ref[...] = jnp.dot(flex_ref[slab(face, size), :], lam, preferred_element_type=F32)


def begin(levels, table_hbm, index_hbm, live_hbm, loads_hbm, coupling_hbm, flex_hbm, *refs):
    bound_ref, limit_ref, weights_ref, flex_ref = refs[:4]
    face_refs = refs[4:8]
    table_ref, index_ref, live_ref, loads_ref, coupling_ref, sems = refs[8:]
    size = face_refs[0].shape[0]
    pairs = [
        (table_hbm, table_ref),
        (index_hbm, index_ref),
        (loads_hbm, loads_ref),
        (live_hbm, live_ref),
        (coupling_hbm, coupling_ref),
    ]
    slabs = [pl.ds(f * size, size) for f in (2, 3, 0, 1)]
    pairs += [(flex_hbm.at[part], flex_ref.at[part]) for part in slabs]
    copies = [
        pltpu.make_async_copy(source, target, sems.at[i])
        for i, (source, target) in enumerate(pairs)
    ]
    for copy in copies:
        copy.start()
    for copy in copies[:3]:
        copy.wait()
    index = index_ref[...]
    row = jnp.zeros(index.shape, F32)
    for level in range(levels):
        row = jnp.where(index == level, table_ref[level], row)
    bound = jnp.transpose(jnp.broadcast_to(row, (loads_ref.shape[1], row.shape[1])))
    bound_ref[...] = bound
    lam = jnp.clip(loads_ref[...].astype(F32), -bound, bound).astype(BF16)
    for copy in copies[3:5]:
        copy.wait()
    for k, face in enumerate(face_order()):
        limit_ref[k : k + 1, :] = jnp.full((1, limit_ref.shape[1]), live_ref[0, face], jnp.int32)
    corners, _, length = coupling_ref.shape
    padded = weights_ref.shape[0] // 3
    coupling = coupling_ref[...].reshape(corners, length)
    if padded > corners:
        rest = jnp.zeros((padded - corners, length), F32)
        coupling = jnp.concatenate([coupling, rest], axis=0)
    high, low = halves(coupling)
    weights_ref[...] = jnp.concatenate([high, low, high], axis=0)
    for half in (slice(0, 2), slice(2, 4)):
        for copy in copies[5:][half]:
            copy.wait()
        for face, ref in list(zip(face_order(), face_refs))[half]:
            ref[...] = jnp.dot(flex_ref[slab(face, size), :], lam, preferred_element_type=F32)


def stepped(sums_ref, lam, search_ref, bound):
    sums = jnp.sum(sums_ref[...], axis=0)
    return jnp.clip(lam - (sums[0:1] / sums[1:2]) * search_ref[...], -bound, bound)


def again(sums_ref, loads_ref, search_ref, bound_ref, flex_ref, lam_ref, *face_refs):
    bound = bound_ref[...]
    lam = jnp.clip(loads_ref[...].astype(F32), -bound, bound)
    lam = stepped(sums_ref, lam, search_ref, bound)
    lam_ref[...] = lam
    put_faces(flex_ref, lam.astype(BF16), face_refs)


def end(sums_ref, lam_ref, search_ref, bound_ref, out_ref):
    out_ref[...] = stepped(sums_ref, lam_ref[...], search_ref, bound_ref[...]).astype(BF16)


def own_rows(block_refs, mine_ref):
    rows = len(block_refs)
    corners = block_refs[0].shape[0] // rows
    padded, lanes = mine_ref.shape[0] // 2, mine_ref.shape[1] // rows
    here = lax.axis_index("row")
    mine_ref[...] = jnp.zeros(mine_ref.shape, BF16)
    for k, ref in enumerate(block_refs):
        chosen = ref[0:corners, :]
        for r in range(1, rows):
            chosen = jnp.where(here == r, ref[r * corners : (r + 1) * corners, :], chosen)
        at = slice(k * lanes, k * lanes + chosen.shape[1])
        high, low = halves(chosen)
        mine_ref[0:corners, at] = high
        mine_ref[padded : padded + corners, at] = low


def jumps(blocks, limit_ref, loads_ref, weights_ref, *refs):
    faces, paired, block_refs = refs[:4], refs[4:8], refs[8 : 8 + blocks]
    jump_ref, force_ref, *mine_refs = refs[8 + blocks :]
    if blocks:
        own_rows(block_refs, *mine_refs)
    size = faces[0].shape[0]
    slot = lax.broadcasted_iota(jnp.int32, faces[0].shape, 0)
    for k, face in enumerate(face_order()):
        at = slab(face, size)
        part = faces[k][...] - paired[k][...] - loads_ref[at, :].astype(F32)
        jump_ref[at, :] = jnp.where(slot < limit_ref[k : k + 1, :], part, 0.0)
    jump = jump_ref[...]
    _, groups, group, width = force_ref.shape
    padded = weights_ref.shape[0] // 3
    high, low = halves(jump)
    force = two_part_dot(weights_ref.at[0 : 2 * padded], high, low)
    force = force[: groups * group].reshape(1, groups, group, width)
    force_ref[...] = jnp.broadcast_to(force, force_ref.shape)


def directions(
    blocks, forces_ref, mine_ref, weights_ref, jump_ref, schur_ref, flex_ref, *refs
):
    search_ref, sums_ref, ordered_ref = refs[:3]
    count, groups, group, width = forces_ref.shape
    rows = blocks
    lanes = mine_ref.shape[1] // blocks
    corners = groups * group
    span = count * corners // blocks
    cols = count // rows
    if lanes > span:
        for b in range(blocks):
            ordered_ref[b, span:, :] = jnp.zeros((lanes - span, width), F32)
    for r in range(rows):
        for c in range(cols):
            start = (c * rows + r) * corners
            for g in range(groups):
                at = start % span + g * group
                ordered_ref[start // span, at : at + group, :] = forces_ref[r * cols + c, g]
    here = lax.axis_index("row")
    sources = [partner(here, rows, rows - k if rows & (rows - 1) else k) for k in range(rows)]
    high, low = halves(jnp.concatenate([ordered_ref[source] for source in sources], axis=0))
    coarse = two_part_dot(mine_ref, high, low)
    high, low = halves(coarse)
    correction = lax.dot_general(
        weights_ref[...],
        jnp.concatenate([high, high, low], axis=0),
        (((0,), (0,)), ((), ())),
        preferred_element_type=F32,
    )
    projected_ref, along_ref = refs[3:]
    projected_ref[...] = (jump_ref[...] - correction).astype(BF16)
    size = jump_ref.shape[0] // 2
    slabs = [slice(at, at + size) for at in range(0, jump_ref.shape[0], size)]
    gain = curvature = jnp.zeros((1, width), F32)
    projected = projected_ref[...]
    for at in slabs:
        search = jnp.dot(schur_ref[at, :], projected, preferred_element_type=F32)
        search_ref[at, :] = search
        along_ref[at, :] = search.astype(BF16)
        gain += jnp.sum(projected_ref[at, :].astype(F32) * search, axis=0, keepdims=True)
    along = along_ref[...]
    for at in slabs:
        curved = jnp.dot(flex_ref[at, :], along, preferred_element_type=F32)
        curvature += jnp.sum(along_ref[at, :].astype(F32) * curved, axis=0, keepdims=True)
    sums = jnp.concatenate([gain, curvature], axis=0)
    sums_ref[...] = jnp.broadcast_to(sums[None], sums_ref.shape)


def local(
    slip_load,
    flexibility,
    schur,
    corner_coupling,
    coarse_inverse,
    bounds_table,
    bound_index,
    face_rows,
):
    loads = slip_load[0, 0]
    flex = flexibility[0, 0]
    shell = schur[0, 0]
    coupling = corner_coupling[0, 0][:, None, :]
    row_count, width = loads.shape
    face = ((row_count // 4, width), F32)
    whole = ((row_count, width), F32)
    rows, cols = lax.axis_size("row"), lax.axis_size("col")
    count = rows * cols
    corners = coupling.shape[0]
    group = 4 if corners % 4 == 0 else 1
    shared = ((count, corners // group, group, width), F32)
    padded = -(-corners // 8) * 8
    lanes = -(-coarse_inverse.shape[0] // 128) * 128
    work = 2 * row_count * row_count * width

    def exchanged(blocks):
        return lax.all_to_all(blocks, ALL, 0, 0, tiled=True)

    block = coarse_inverse.T
    blocks = [block]
    for k in range(1, rows):
        to = [partner(r, rows, k) for r in range(rows)]
        blocks.append(passed(block, "row", to))
    inputs = (
        bounds_table,
        bound_index[0],
        face_rows[0],
        loads,
        coupling,
        flex,
    )
    outs = kernel_call(
        functools.partial(begin, bounds_table.shape[0]),
        [HBM] * 6,
        [
            whole,
            ((8, width), jnp.int32),
            ((3 * padded, row_count), BF16),
            (flex.shape, BF16),
        ]
        + [face] * 4,
        work,
        [
            pltpu.SMEM(bounds_table.shape, F32),
            pltpu.VMEM((1, row_count), jnp.int32),
            pltpu.SMEM((1, 4), jnp.int32),
            pltpu.VMEM(loads.shape, BF16),
            pltpu.VMEM(coupling.shape, F32),
            pltpu.SemaphoreType.DMA((9,)),
        ],
    )(*(in_hbm(x) for x in inputs))
    bound, limit, weights, flex = outs[:4]
    faces = outs[4:]
    for iteration in range(ITERS):
        paired = across(faces)
        if iteration == 0:
            paired[0], *blocks = lax.optimization_barrier((paired[0], *blocks))
            jump, forces, mine = kernel_call(
                functools.partial(jumps, rows),
                [VMEM] * (11 + rows),
                [whole, shared, ((2 * padded, rows * lanes), BF16)],
                work // 8,
            )(limit, loads, weights, *faces, *paired, *blocks)
        else:
            jump, forces = kernel_call(
                functools.partial(jumps, 0), [VMEM] * 11, [whole, shared], work // 8
            )(limit, loads, weights, *faces, *paired)
        forces = exchanged(forces)
        search, sums = kernel_call(
            functools.partial(directions, rows),
            [VMEM] * 6,
            [whole, ((count, 2, width), F32)],
            2 * work,
            [
                pltpu.VMEM((rows, lanes, width), F32),
                pltpu.VMEM((row_count, width), BF16),
                pltpu.VMEM((row_count, width), BF16),
            ],
        )(forces, mine, weights, jump, shell, flex)
        sums = exchanged(sums)
        if iteration < ITERS - 1:
            lam, *faces = kernel_call(
                again, [VMEM] * 5, [whole] + [face] * 4, work
            )(sums, loads, search, bound, flex)
        else:
            (out,) = kernel_call(
                end, [VMEM] * 4, [((row_count, width), BF16)], work // 64
            )(sums, lam, search, bound)
    return out[None, None]


def solution(mesh):
    return jax.shard_map(
        local,
        mesh=mesh,
        in_specs=(
            P("row", "col", None, None),
            P("row", "col", None, None),
            P("row", "col", None, None),
            P("row", "col", None, None),
            P("row", "col"),
            P(),
            P("row", "col", None),
            P("row", "col", None),
        ),
        out_specs=P("row", "col", None, None),
        check_vma=False,
    )
```
